32 devices in a mesh: groups: 2 (over y), tm: 8 (over z, x), space: 2 (over core).
Axes of the slice: x: 2, y: 2, z: 4, core: 2. Of those that a mesh axis runs over, the one named last changes fastest.
Arguments:
- latent: bfloat16 [32, 16, 32, 256], P(('groups', 'tm'), 'space'), parts along dimension 0, may hold values from -6 to 6
- first_kernel: bfloat16 [256, 27, 256], P('tm'), may hold values from -0.078125 to 0.078125
- second_kernel: bfloat16 [256, 27, 128], P('tm'), may hold values from -0.078125 to 0.078125
Outputs:
- decoded: bfloat16 [32, 32, 64, 128], P(('groups', 'tm'), 'space'), parts along dimension 0
The draws below stay inside these ranges and needn't reach their ends.
There are 2 independent parts, one for each index of `groups`. The reference program is written for one: setup_inputs(seed, part) draws one part's arguments, and reference() takes and returns one part's arrays. A program takes and returns all parts, laid end to end along the dimension named above; an argument that names none is the same for every part. Nothing has to cross between parts.
All inputs are finite; a program needn't handle non-finite values.
Results may differ from the reference program's by a relative error of at most 0.005.
Values may be sent and summed in bfloat16 or wider, within the bound.
A program may use at most 64 MiB of HBM per device.

```python
import jax
import jax.numpy as jnp
from jax import lax

C1 = 256
C2 = 128
WIDTH = 32
FRAMES = 16
ROWS = 16


def levels(own_key, shape, shards, smallest, high):
    def one(dim, blocks):
        steps = jax.random.uniform(jax.random.fold_in(jax.random.fold_in(own_key, 6), dim), (blocks,), jnp.float32, smallest / len(shards), high / len(shards))
        return jnp.repeat(jnp.exp(steps), shape[dim] // blocks).reshape((-1,) + (1,) * (len(shape) - dim - 1))

    factor_of = one(*shards[0])
    for cut in shards[1:]:
        factor_of = factor_of * one(*cut)
    return factor_of


def scatter_about(own_key, extent, deviation, reach, cuts=(), kind=jnp.bfloat16):
    entries = deviation * jax.random.normal(own_key, extent, jnp.float32)
    if cuts:
        entries = entries * levels(own_key, extent, cuts, -0.22, 0.18)
    return jnp.clip(entries, -reach, reach).astype(kind)


def setup_inputs(seed: int = 0, part: int = 0) -> dict:
    splits = jax.random.split(jax.random.key(seed), 4)
    part_splits = jax.random.split(jax.random.fold_in(splits[3], part), 4)
    latent = scatter_about(part_splits[0], (FRAMES, ROWS, WIDTH, C1), 1.0, 6.0, ((0, 8), (1, 2)))
    first_kernel = scatter_about(splits[1], (C1, 27, C1), (27 * C1) ** -0.5, 0.078125, ((0, 8),))
    second_kernel = scatter_about(splits[2], (C1, 27, C2), (27 * C1) ** -0.5, 0.078125, ((0, 8),))
    return dict(latent=latent, first_kernel=first_kernel, second_kernel=second_kernel)


def conv_block(padded, kernel):
    channels = kernel.shape[0]
    outputs = kernel.shape[2]
    filters = kernel.reshape(channels, 3, 3, 3, outputs).transpose(1, 2, 3, 0, 4)
    result = lax.conv_general_dilated(padded[None], filters, (1, 1, 1), ((0, 0), (0, 0), (1, 1)), dimension_numbers=("NDHWC", "DHWIO", "NDHWC"), preferred_element_type=jnp.float32)
    return result[0]


def upsample(field):
    return jnp.repeat(jnp.repeat(field, 2, axis=1), 2, axis=2)


def reference(latent, first_kernel, second_kernel):
    padded = jnp.pad(latent, ((2, 0), (1, 1), (0, 0), (0, 0)))
    pre = conv_block(padded, first_kernel)
    hidden = jax.nn.silu(pre).astype(jnp.bfloat16)
    larger = jnp.pad(upsample(hidden), ((2, 0), (1, 1), (0, 0), (0, 0)))
    return conv_block(larger, second_kernel).astype(jnp.bfloat16)
```

```python
import functools

import jax
import jax.numpy as jnp
from jax import lax
from jax.experimental import pallas as pl
from jax.experimental.pallas import tpu as pltpu
from jax.sharding import PartitionSpec as P

MESH = pl.DeviceIdType.MESH
F32 = jnp.float32
BF16 = jnp.bfloat16


def shifted(x, axis, by):
    count = lax.axis_size(axis)
    pairs = [(i, i + by) for i in range(count) if 0 <= i + by < count]
    return lax.ppermute(x, axis, pairs)


def padded_2(x, sides, width):
    for axis, dim in sides:
        count, length = (lax.axis_size(axis), x.shape[dim])
        up = [(i, (i + 1) % count) for i in range(count - 1)]
        down = [(j, i) for i, j in up]
        last = lax.slice_in_dim(x, length - width, length, axis=dim)
        leading = lax.slice_in_dim(x, 0, width, axis=dim)
        before = lax.ppermute(last, axis, up)
        after = lax.ppermute(leading, axis, down)
        x = jnp.concatenate([before, x, after], axis=dim)
    return x


def conv_block(padded, kernel):
    channels = kernel.shape[0]
    outputs = kernel.shape[2]
    filters = kernel.reshape(channels, 3, 3, 3, outputs).transpose(1, 2, 3, 0, 4)
    result = lax.conv_general_dilated(
        padded[None],
        filters,
        (1, 1, 1),
        ((0, 0), (0, 0), (1, 1)),
        dimension_numbers=("NDHWC", "DHWIO", "NDHWC"),
        preferred_element_type=jnp.float32,
    )
    return result[0]


def upsample(field):
    return jnp.repeat(jnp.repeat(field, 2, axis=1), 2, axis=2)


def plain(latent, first_kernel, second_kernel):
    frames = latent.shape[0]
    extended = jnp.concatenate([shifted(latent[frames - 2 :], "tm", 1), latent], 0)
    padded = padded_2(extended, (("space", 1),), 1)
    pre = conv_block(padded, lax.all_gather(first_kernel, "tm", axis=0, tiled=True))
    hidden = jax.nn.silu(pre).astype(BF16)
    hidden_ext = jnp.concatenate([shifted(hidden[frames - 2 :], "tm", 1), hidden], 0)
    larger = padded_2(upsample(hidden_ext), (("space", 1),), 1)
    piece = lax.all_gather(second_kernel, "tm", axis=0, tiled=True)
    return conv_block(larger, piece).astype(BF16)


def roll_cols(x, by, width):
    rows = x.shape[0]
    col = lax.broadcasted_iota(jnp.int32, x.shape, 0) % width
    if by == 1:
        return jnp.where(col == 0, 0.0, pltpu.roll(x, 1, 0))
    return jnp.where(col == width - 1, 0.0, pltpu.roll(x, rows - 1, 0))


def kernel(
    n, latent, k1, k2, out,
    b1, b2, x, h, v, acc, wide,
    own_sem, lat_send, lat_recv, hid_send, hid_recv,
    ring1, ring2, yrec1, yrec2, ring_send, y_send, sib_send, sibf_send, sib1, sib2, sibf1, sibf2,
):
    y = lax.axis_index("groups")
    tm = lax.axis_index("tm")
    c = lax.axis_index("space")
    half = n // 2
    rows, width, c1 = latent.shape[1:]
    c2 = k2.shape[2]
    m = rows * width

    odd = tm % 2
    pos = (1 - odd) * (tm // 2) + odd * (n - 1 - tm // 2)

    def at(p):
        q = (p + 2 * n) % n
        u = q // half
        return (1 - u) * (2 * q) + u * (2 * (n - 1 - q) + 1)

    ring_to = [(y, at(pos + 1), c), (y, at(pos - 1), c)]
    sibling = (y, tm, 1 - c)
    across = (1 - y, tm, c)
    after = (tm + 1) % n
    before = (tm + n - 1) % n

    barrier = pltpu.get_barrier_semaphore()
    partners = ring_to + [sibling, across, (y, after, c), (y, after, 1 - c), (y, before, c), (y, before, 1 - c)]
    for d in partners:
        pl.semaphore_signal(barrier, inc=1, device_id=d, device_id_type=MESH)

    third = 2 * y * (1 - c) + c
    other = 2 * (1 - y)

    def rcopy(src, dst, ss, rs, dev):
        return pltpu.make_async_remote_copy(
            src_ref=src, dst_ref=dst, send_sem=ss, recv_sem=rs, device_id=dev, device_id_type=MESH
        )

    def drain(ref, sem):
        pltpu.make_async_copy(ref, ref, sem).wait()

    own = [
        pltpu.make_async_copy(k1, b1.at[tm], own_sem.at[0]),
        pltpu.make_async_copy(k2, b2.at[tm], own_sem.at[1]),
        pltpu.make_async_copy(latent, x.at[2:4, 1:9], own_sem.at[2]),
    ]
    for o in own:
        o.start()
    zline = jnp.zeros((4, 1, width, c1), BF16)
    x[:, pl.ds(9 * c, 1)] = zline
    h[:, pl.ds(9 * c, 1)] = zline

    @pl.when(tm == 0)
    def _():
        x[0:2] = jnp.zeros((2, 10, width, c1), BF16)
        h[0:2] = jnp.zeros((2, 10, width, c1), BF16)

    pl.semaphore_wait(barrier, len(partners))

    class Gather:
        def __init__(self, src, buf, ring, yrec, sib, sibf, cuts, far, which):
            self.src, self.buf, self.ring, self.yrec = src, buf, ring, yrec
            self.sib, self.sibf, self.cuts, self.far, self.which = sib, sibf, cuts, far, which
            self.size = 9 // cuts

        def taps(self, t, j):
            return pl.ds(t * 9 + self.size * j, self.size)

        def send_own(self):
            for j in range(self.cuts):
                for d in range(2):
                    if self.far[d] >= 1:
                        t = self.taps(third, j)
                        rcopy(self.src.at[t], self.buf.at[tm, t], ring_send.at[self.which], self.ring.at[d, 0, j], ring_to[d]).start()

        def shard(self, d, k):
            return at(pos - k) if d == 0 else at(pos + k)

        def ring_step(self, k):
            for j in range(self.cuts):
                for d in range(2):
                    if k > self.far[d]:
                        continue
                    s = self.shard(d, k)
                    r = self.buf.at[s, self.taps(third, j)]
                    drain(r, self.ring.at[d, k - 1, j])
                    if k < self.far[d]:
                        rcopy(r, r, ring_send.at[self.which], self.ring.at[d, k, j], ring_to[d]).start()
                    rcopy(r, r, sib_send.at[self.which], self.sib, sibling).start()

                    @pl.when(c == 0)
                    def _():
                        rcopy(r, r, y_send.at[self.which], self.yrec.at[d, k - 1, j], across).start()

        def y_step(self, k):
            @pl.when(c == 0)
            def _():
                for j in range(self.cuts):
                    for d in range(2):
                        if k > self.far[d]:
                            continue
                        r = self.buf.at[self.shard(d, k), self.taps(other, j)]
                        drain(r, self.yrec.at[d, k - 1, j])
                        rcopy(r, r, sibf_send.at[self.which], self.sibf, sibling).start()

        def arrive(self):
            drain(self.buf.at[0 : n - 1, 0:9], self.sib)

            @pl.when(c == 1)
            def _():
                drain(self.buf.at[0 : n - 1, 0:9], self.sibf)

        def finish(self):
            ref = self.buf.at[0 : n - 1, 0:9]
            drain(ref, ring_send.at[self.which])
            drain(ref, sib_send.at[self.which])

            @pl.when(c == 0)
            def _():
                drain(ref, y_send.at[self.which])
                drain(ref, sibf_send.at[self.which])

    far = half
    g1 = Gather(k1, b1, ring1, yrec1, sib1, sibf1, 3, (far, n - 1 - far), 0)
    g2 = Gather(k2, b2, ring2, yrec2, sib2, sibf2, 1, (n - 1 - far, far), 1)

    def halo(src, edge, dst, ss, rs, frame):
        f = pl.ds(frame, 1)
        line = pl.ds(9 * c, 1)
        ahead = rcopy(src, dst.at[f, 1:9], ss.at[0, frame], rs.at[0, frame], (y, after, c))
        cross = rcopy(edge, dst.at[pl.ds(frame + 2, 1), line], ss.at[1, frame], rs.at[1, frame], sibling)
        both = rcopy(edge, dst.at[f, line], ss.at[2, frame], rs.at[2, frame], (y, after, 1 - c))
        return ahead, cross, both

    def start_halo(copies):
        ahead, cross, both = copies
        cross.start()

        @pl.when(tm < n - 1)
        def _():
            ahead.start()
            both.start()

    def recv_time(copies):
        ahead, cross, both = copies

        @pl.when(tm > 0)
        def _():
            ahead.wait_recv()

    lat = [halo(latent.at[f : f + 1], latent.at[f : f + 1, pl.ds(7 - 7 * c, 1)], x, lat_send, lat_recv, f) for f in range(2)]
    hid = [halo(h.at[f + 2 : f + 3, 1:9], h.at[f + 2 : f + 3, pl.ds(8 - 7 * c, 1)], h, hid_send, hid_recv, f) for f in range(2)]
    mine = pl.ds(9 - 9 * c, 1)

    def recv_both(dst, rs, frame):
        @pl.when(tm > 0)
        def _():
            drain(dst.at[frame : frame + 1, 1:9], rs.at[0, frame])
            drain(dst.at[frame : frame + 1, mine], rs.at[2, frame])

    def recv_cross(dst, rs, frame):
        drain(dst.at[frame + 2 : frame + 3, mine], rs.at[1, frame])

    g1.send_own()
    for f in range(2):
        start_halo(lat[f])
    for k in range(1, far + 1):
        if k == far:
            g2.send_own()
        g1.ring_step(k)
        if k > 1:
            g1.y_step(k - 1)
    g2.ring_step(1)
    g1.y_step(far)
    for o in own:
        o.wait()
    g1.arrive()
    for f in range(2):
        recv_both(x, lat_recv, f)
        recv_cross(x, lat_recv, f)

    def slab(ref, f, r):
        return ref[f, r : r + 8].reshape(m, c1)

    def weight(dt, dr, dc):
        return b1[:, 9 * dt + 3 * dr + dc].reshape(c1, b1.shape[3])

    def conv1(f):
        lhs = jnp.concatenate([slab(x, f + dt, dr) for dt in range(3) for dr in range(3)], axis=1)
        parts = []
        for dc in range(3):
            rhs = jnp.concatenate([weight(dt, dr, dc) for dt in range(3) for dr in range(3)], axis=0)
            parts.append(jnp.dot(lhs, rhs, preferred_element_type=F32))
        pre = roll_cols(parts[0], 1, width) + parts[1] + roll_cols(parts[2], -1, width)
        val = pre / (1.0 + jnp.exp(-pre))
        h[f + 2, 1:9] = val.astype(BF16).reshape(rows, width, c1)

    conv1(0)
    start_halo(hid[0])
    g2.ring_step(2)
    g2.y_step(1)
    conv1(1)
    start_halo(hid[1])
    for k in range(3, far + 1):
        g2.ring_step(k)
        g2.y_step(k - 1)
    g2.y_step(far)
    g2.arrive()

    for dt in range(3):
        w = [[b2[:, 9 * dt + 3 * dr + dc].reshape(c1, c2).astype(F32) for dc in range(3)] for dr in range(3)]
        lines = [
            [w[0], [w[1][i] + w[2][i] for i in range(3)]],
            [[w[0][i] + w[1][i] for i in range(3)], w[2]],
        ]
        for pr in range(2):
            for ro in range(2):
                a = lines[pr][ro]
                v[pr, 2 * dt + ro] = jnp.concatenate([a[0], a[2], a[1] + a[2], a[0] + a[1]], axis=1).astype(BF16)

    def term(f, pr, dts):
        lhs = jnp.concatenate([slab(h, f + dt, pr + ro) for dt in dts for ro in range(2)], axis=1)
        rhs = v[pr, 2 * dts[0] : 2 * dts[-1] + 2].reshape(2 * len(dts) * c1, 4 * c2)
        return jnp.dot(lhs, rhs, preferred_element_type=F32)

    for f in range(2):
        recv_cross(h, hid_recv, f)
    early = [(2,), (1, 2)]
    late = [(0, 1), (0,)]
    for f in range(2):
        for pr in range(2):
            acc[f, pr] = term(f, pr, early[f])
    for f in range(2):
        recv_both(h, hid_recv, f)
    for f in range(2):
        for pr in range(2):
            p = acc[f, pr] + term(f, pr, late[f])
            left = roll_cols(p[:, 0:c2], 1, width) + p[:, 2 * c2 : 3 * c2]
            right = p[:, 3 * c2 : 4 * c2] + roll_cols(p[:, c2 : 2 * c2], -1, width)
            wide[pl.ds(0, m, stride=2)] = left
            wide[pl.ds(1, m, stride=2)] = right
            res = wide[...].astype(BF16).reshape(rows, 2 * width, c2)
            for r in range(rows):
                out[f, 2 * r + pr] = res[r]

    g1.finish()
    g2.finish()
    for copies in lat + hid:
        ahead, cross, both = copies
        cross.wait_send()

        @pl.when(tm < n - 1)
        def _():
            ahead.wait_send()
            both.wait_send()


def fused(n, latent, first_kernel, second_kernel):
    frames, rows, width, c1 = latent.shape
    ch, _, o1 = first_kernel.shape
    c2 = second_kernel.shape[2]
    k1 = first_kernel.transpose(1, 0, 2)
    k2 = second_kernel.transpose(1, 0, 2)
    far = n // 2
    dma = pltpu.SemaphoreType.DMA
    vm = pl.BlockSpec(memory_space=pltpu.VMEM)
    m = rows * width
    return pl.pallas_call(
        functools.partial(kernel, n),
        out_shape=jax.ShapeDtypeStruct((frames, 2 * rows, 2 * width, c2), BF16),
        in_specs=[vm] * 3,
        out_specs=vm,
        scratch_shapes=[
            pltpu.VMEM((n, 27, ch, o1), BF16),
            pltpu.VMEM((n, 27, ch, c2), BF16),
            pltpu.VMEM((4, rows + 2, width, c1), BF16),
            pltpu.VMEM((4, rows + 2, width, o1), BF16),
            pltpu.VMEM((2, 6, o1, 4 * c2), BF16),
            pltpu.VMEM((2, 2, m, 4 * c2), F32),
            pltpu.VMEM((2 * m, c2), F32),
            dma((3,)), dma((3, 2)), dma((3, 2)), dma((3, 2)), dma((3, 2)),
            dma((2, far, 3)), dma((2, far, 1)), dma((2, far, 3)), dma((2, far, 1)),
            dma((2,)), dma((2,)), dma((2,)), dma((2,)), dma, dma, dma, dma,
        ],
        compiler_params=pltpu.CompilerParams(
            collective_id=0, has_side_effects=True, vmem_limit_bytes=58 * 1024 * 1024
        ),
    )(latent, k1, k2)


def solution(mesh):
    n = mesh.shape["tm"]

    def shards(latent, first_kernel, second_kernel):
        ch = first_kernel.shape[0]
        fits = (
            ch % 16 == 0 and n % 2 == 0 and n >= 4 and latent.shape[:2] == (2, 8)
            and mesh.shape["space"] == 2 and mesh.shape["groups"] == 2
        )
        if fits:
            return fused(n, latent, first_kernel, second_kernel)
        return plain(latent, first_kernel, second_kernel)

    in_specs = (P(("groups", "tm"), "space", None, None), P("tm", None, None), P("tm", None, None))
    out_specs = P(("groups", "tm"), "space", None, None)
    return jax.shard_map(shards, mesh=mesh, in_specs=in_specs, out_specs=out_specs, check_vma=False)
```

```python
import functools

import jax
import jax.numpy as jnp
from jax import lax
from jax.experimental import pallas as pl
from jax.experimental.pallas import tpu as pltpu
from jax.sharding import PartitionSpec as P

MESH = pl.DeviceIdType.MESH
F32 = jnp.float32
BF16 = jnp.bfloat16


def shifted(x, axis, by):
    count = lax.axis_size(axis)
    pairs = [(i, i + by) for i in range(count) if 0 <= i + by < count]
    return lax.ppermute(x, axis, pairs)


def padded_2(x, sides, width):
    for axis, dim in sides:
        count, length = (lax.axis_size(axis), x.shape[dim])
        up = [(i, (i + 1) % count) for i in range(count - 1)]
        down = [(j, i) for i, j in up]
        last = lax.slice_in_dim(x, length - width, length, axis=dim)
        leading = lax.slice_in_dim(x, 0, width, axis=dim)
        before = lax.ppermute(last, axis, up)
        after = lax.ppermute(leading, axis, down)
        x = jnp.concatenate([before, x, after], axis=dim)
    return x


def conv_block(padded, kernel):
    channels = kernel.shape[0]
    outputs = kernel.shape[2]
    filters = kernel.reshape(channels, 3, 3, 3, outputs).transpose(1, 2, 3, 0, 4)
    result = lax.conv_general_dilated(
        padded[None],
        filters,
        (1, 1, 1),
        ((0, 0), (0, 0), (1, 1)),
        dimension_numbers=("NDHWC", "DHWIO", "NDHWC"),
        preferred_element_type=jnp.float32,
    )
    return result[0]


def upsample(field):
    return jnp.repeat(jnp.repeat(field, 2, axis=1), 2, axis=2)


def plain(latent, first_kernel, second_kernel):
    frames = latent.shape[0]
    extended = jnp.concatenate([shifted(latent[frames - 2 :], "tm", 1), latent], 0)
    padded = padded_2(extended, (("space", 1),), 1)
    pre = conv_block(padded, lax.all_gather(first_kernel, "tm", axis=0, tiled=True))
    hidden = jax.nn.silu(pre).astype(BF16)
    hidden_ext = jnp.concatenate([shifted(hidden[frames - 2 :], "tm", 1), hidden], 0)
    larger = padded_2(upsample(hidden_ext), (("space", 1),), 1)
    piece = lax.all_gather(second_kernel, "tm", axis=0, tiled=True)
    return conv_block(larger, piece).astype(BF16)


def roll_cols(x, by, width):
    rows = x.shape[0]
    col = lax.broadcasted_iota(jnp.int32, x.shape, 0) % width
    if by == 1:
        return jnp.where(col == 0, 0.0, pltpu.roll(x, 1, 0))
    return jnp.where(col == width - 1, 0.0, pltpu.roll(x, rows - 1, 0))


def kernel(
    n, latent, k1, k2, out,
    b1, b2, x, h, v, acc, wide,
    own_sem, lat_send, lat_recv, hid_send, hid_recv,
    ring1, ring2, yrec1, yrec2, ring_send, y_send, sib_send, sibf_send, sib1, sib2, sibf1, sibf2,
):
    y = lax.axis_index("groups")
    tm = lax.axis_index("tm")
    c = lax.axis_index("space")
    half = n // 2
    rows, width, c1 = latent.shape[1:]
    c2 = k2.shape[2]
    m = rows * width

    odd = tm % 2
    pos = (1 - odd) * (tm // 2) + odd * (n - 1 - tm // 2)

    def at(p):
        q = (p + 2 * n) % n
        u = q // half
        return (1 - u) * (2 * q) + u * (2 * (n - 1 - q) + 1)

    ring_to = [(y, at(pos + 1), c), (y, at(pos - 1), c)]
    sibling = (y, tm, 1 - c)
    across = (1 - y, tm, c)
    after = (tm + 1) % n
    before = (tm + n - 1) % n

    barrier = pltpu.get_barrier_semaphore()
    partners = ring_to + [sibling, across, (y, after, c), (y, after, 1 - c), (y, before, c), (y, before, 1 - c)]
    for d in partners:
        pl.semaphore_signal(barrier, inc=1, device_id=d, device_id_type=MESH)

    third = 2 * y * (1 - c) + c
    other = 2 * (1 - y)

    def rcopy(src, dst, ss, rs, dev):
        return pltpu.make_async_remote_copy(
            src_ref=src, dst_ref=dst, send_sem=ss, recv_sem=rs, device_id=dev, device_id_type=MESH
        )

    def drain(ref, sem):
        pltpu.make_async_copy(ref, ref, sem).wait()

    own = [
        pltpu.make_async_copy(k1, b1.at[tm], own_sem.at[0]),
        pltpu.make_async_copy(k2, b2.at[tm], own_sem.at[1]),
        pltpu.make_async_copy(latent, x.at[2:4, 1:9], own_sem.at[2]),
    ]
    for o in own:
        o.start()
    zline = jnp.zeros((4, 1, width, c1), BF16)
    x[:, pl.ds(9 * c, 1)] = zline
    h[:, pl.ds(9 * c, 1)] = zline

    @pl.when(tm == 0)
    def _():
        x[0:2] = jnp.zeros((2, 10, width, c1), BF16)
        h[0:2] = jnp.zeros((2, 10, width, c1), BF16)

    pl.semaphore_wait(barrier, len(partners))

    class Gather:
        def __init__(self, src, buf, ring, yrec, sib, sibf, cuts, far, which):
            self.src, self.buf, self.ring, self.yrec = src, buf, ring, yrec
            self.sib, self.sibf, self.cuts, self.far, self.which = sib, sibf, cuts, far, which
            self.size = 9 // cuts

        def taps(self, t, j):
            return pl.ds(t * 9 + self.size * j, self.size)

        def send_own(self):
            for j in range(self.cuts):
                for d in range(2):
                    if self.far[d] >= 1:
                        t = self.taps(third, j)
                        rcopy(self.src.at[t], self.buf.at[tm, t], ring_send.at[self.which], self.ring.at[d, 0, j], ring_to[d]).start()

        def shard(self, d, k):
            return at(pos - k) if d == 0 else at(pos + k)

        def ring_step(self, k):
            for j in range(self.cuts):
                for d in range(2):
                    if k > self.far[d]:
                        continue
                    s = self.shard(d, k)
                    r = self.buf.at[s, self.taps(third, j)]
                    drain(r, self.ring.at[d, k - 1, j])
                    if k < self.far[d]:
                        rcopy(r, r, ring_send.at[self.which], self.ring.at[d, k, j], ring_to[d]).start()
                    rcopy(r, r, sib_send.at[self.which], self.sib, sibling).start()

                    @pl.when(c == 0)
                    def _():
                        rcopy(r, r, y_send.at[self.which], self.yrec.at[d, k - 1, j], across).start()

        def y_step(self, k):
            @pl.when(c == 0)
            def _():
                for j in range(self.cuts):
                    for d in range(2):
                        if k > self.far[d]:
                            continue
                        r = self.buf.at[self.shard(d, k), self.taps(other, j)]
                        drain(r, self.yrec.at[d, k - 1, j])
                        rcopy(r, r, sibf_send.at[self.which], self.sibf, sibling).start()

        def arrive(self):
            drain(self.buf.at[0 : n - 1, 0:9], self.sib)

            @pl.when(c == 1)
            def _():
                drain(self.buf.at[0 : n - 1, 0:9], self.sibf)

        def finish(self):
            ref = self.buf.at[0 : n - 1, 0:9]
            drain(ref, ring_send.at[self.which])
            drain(ref, sib_send.at[self.which])

            @pl.when(c == 0)
            def _():
                drain(ref, y_send.at[self.which])
                drain(ref, sibf_send.at[self.which])

    far = half
    g1 = Gather(k1, b1, ring1, yrec1, sib1, sibf1, 3, (far, n - 1 - far), 0)
    g2 = Gather(k2, b2, ring2, yrec2, sib2, sibf2, 3, (n - 1 - far, far), 1)

    def halo(src, edge, dst, ss, rs, frame):
        f = pl.ds(frame, 1)
        line = pl.ds(9 * c, 1)
        ahead = rcopy(src, dst.at[f, 1:9], ss.at[0, frame], rs.at[0, frame], (y, after, c))
        cross = rcopy(edge, dst.at[pl.ds(frame + 2, 1), line], ss.at[1, frame], rs.at[1, frame], sibling)
        both = rcopy(edge, dst.at[f, line], ss.at[2, frame], rs.at[2, frame], (y, after, 1 - c))
        return ahead, cross, both

    def start_halo(copies):
        ahead, cross, both = copies
        cross.start()

        @pl.when(tm < n - 1)
        def _():
            ahead.start()
            both.start()

    def recv_time(copies):
        ahead, cross, both = copies

        @pl.when(tm > 0)
        def _():
            ahead.wait_recv()

    lat = [halo(latent.at[f : f + 1], latent.at[f : f + 1, pl.ds(7 - 7 * c, 1)], x, lat_send, lat_recv, f) for f in range(2)]
    hid = [halo(h.at[f + 2 : f + 3, 1:9], h.at[f + 2 : f + 3, pl.ds(8 - 7 * c, 1)], h, hid_send, hid_recv, f) for f in range(2)]
    mine = pl.ds(9 - 9 * c, 1)

    def recv_both(dst, rs, frame):
        @pl.when(tm > 0)
        def _():
            drain(dst.at[frame : frame + 1, 1:9], rs.at[0, frame])
            drain(dst.at[frame : frame + 1, mine], rs.at[2, frame])

    def recv_cross(dst, rs, frame):
        drain(dst.at[frame + 2 : frame + 3, mine], rs.at[1, frame])

    g1.send_own()
    for f in range(2):
        start_halo(lat[f])
    for k in range(1, far + 1):
        if k == far:
            g2.send_own()
        g1.ring_step(k)
        if k > 1:
            g1.y_step(k - 1)
    g2.ring_step(1)
    g1.y_step(far)
    for o in own:
        o.wait()
    g1.arrive()
    for f in range(2):
        recv_both(x, lat_recv, f)
        recv_cross(x, lat_recv, f)

    def slab(ref, f, r):
        return ref[f, r : r + 8].reshape(m, c1)

    def weight(dt, dr, dc):
        return b1[:, 9 * dt + 3 * dr + dc].reshape(c1, b1.shape[3])

    def conv1(f):
        lhs = jnp.concatenate([slab(x, f + dt, dr) for dt in range(3) for dr in range(3)], axis=1)
        parts = []
        for dc in range(3):
            rhs = jnp.concatenate([weight(dt, dr, dc) for dt in range(3) for dr in range(3)], axis=0)
            parts.append(jnp.dot(lhs, rhs, preferred_element_type=F32))
        pre = roll_cols(parts[0], 1, width) + parts[1] + roll_cols(parts[2], -1, width)
        val = pre / (1.0 + jnp.exp(-pre))
        h[f + 2, 1:9] = val.astype(BF16).reshape(rows, width, c1)

    conv1(0)
    start_halo(hid[0])
    g2.ring_step(2)
    g2.y_step(1)
    conv1(1)
    start_halo(hid[1])
    for k in range(3, far + 1):
        g2.ring_step(k)
        g2.y_step(k - 1)
    g2.y_step(far)
    g2.arrive()

    for dt in range(3):
        w = [[b2[:, 9 * dt + 3 * dr + dc].reshape(c1, c2).astype(F32) for dc in range(3)] for dr in range(3)]
        lines = [
            [w[0], [w[1][i] + w[2][i] for i in range(3)]],
            [[w[0][i] + w[1][i] for i in range(3)], w[2]],
        ]
        for pr in range(2):
            for ro in range(2):
                a = lines[pr][ro]
                v[pr, 2 * dt + ro] = jnp.concatenate([a[0], a[2], a[1] + a[2], a[0] + a[1]], axis=1).astype(BF16)

    def term(f, pr, dts):
        lhs = jnp.concatenate([slab(h, f + dt, pr + ro) for dt in dts for ro in range(2)], axis=1)
        rhs = v[pr, 2 * dts[0] : 2 * dts[-1] + 2].reshape(2 * len(dts) * c1, 4 * c2)
        return jnp.dot(lhs, rhs, preferred_element_type=F32)

    for f in range(2):
        recv_cross(h, hid_recv, f)
    early = [(2,), (1, 2)]
    late = [(0, 1), (0,)]
    for f in range(2):
        for pr in range(2):
            acc[f, pr] = term(f, pr, early[f])
    for f in range(2):
        recv_both(h, hid_recv, f)
    for f in range(2):
        for pr in range(2):
            p = acc[f, pr] + term(f, pr, late[f])
            left = roll_cols(p[:, 0:c2], 1, width) + p[:, 2 * c2 : 3 * c2]
            right = p[:, 3 * c2 : 4 * c2] + roll_cols(p[:, c2 : 2 * c2], -1, width)
            wide[pl.ds(0, m, stride=2)] = left
            wide[pl.ds(1, m, stride=2)] = right
            res = wide[...].astype(BF16).reshape(rows, 2 * width, c2)
            for r in range(rows):
                out[f, 2 * r + pr] = res[r]

    g1.finish()
    g2.finish()
    for copies in lat + hid:
        ahead, cross, both = copies
        cross.wait_send()

        @pl.when(tm < n - 1)
        def _():
            ahead.wait_send()
            both.wait_send()


def fused(n, latent, first_kernel, second_kernel):
    frames, rows, width, c1 = latent.shape
    ch, _, o1 = first_kernel.shape
    c2 = second_kernel.shape[2]
    k1 = first_kernel.transpose(1, 0, 2)
    k2 = second_kernel.transpose(1, 0, 2)
    far = n // 2
    dma = pltpu.SemaphoreType.DMA
    vm = pl.BlockSpec(memory_space=pltpu.VMEM)
    m = rows * width
    return pl.pallas_call(
        functools.partial(kernel, n),
        out_shape=jax.ShapeDtypeStruct((frames, 2 * rows, 2 * width, c2), BF16),
        in_specs=[vm] * 3,
        out_specs=vm,
        scratch_shapes=[
            pltpu.VMEM((n, 27, ch, o1), BF16),
            pltpu.VMEM((n, 27, ch, c2), BF16),
            pltpu.VMEM((4, rows + 2, width, c1), BF16),
            pltpu.VMEM((4, rows + 2, width, o1), BF16),
            pltpu.VMEM((2, 6, o1, 4 * c2), BF16),
            pltpu.VMEM((2, 2, m, 4 * c2), F32),
            pltpu.VMEM((2 * m, c2), F32),
            dma((3,)), dma((3, 2)), dma((3, 2)), dma((3, 2)), dma((3, 2)),
            dma((2, far, 3)), dma((2, far, 3)), dma((2, far, 3)), dma((2, far, 3)),
            dma((2,)), dma((2,)), dma((2,)), dma((2,)), dma, dma, dma, dma,
        ],
        compiler_params=pltpu.CompilerParams(
            collective_id=0, has_side_effects=True, vmem_limit_bytes=58 * 1024 * 1024
        ),
    )(latent, k1, k2)


def solution(mesh):
    n = mesh.shape["tm"]

    def shards(latent, first_kernel, second_kernel):
        ch = first_kernel.shape[0]
        fits = (
            ch % 16 == 0 and n % 2 == 0 and n >= 4 and latent.shape[:2] == (2, 8)
            and mesh.shape["space"] == 2 and mesh.shape["groups"] == 2
        )
        if fits:
            return fused(n, latent, first_kernel, second_kernel)
        return plain(latent, first_kernel, second_kernel)

    in_specs = (P(("groups", "tm"), "space", None, None), P("tm", None, None), P("tm", None, None))
    out_specs = P(("groups", "tm"), "space", None, None)
    return jax.shard_map(shards, mesh=mesh, in_specs=in_specs, out_specs=out_specs, check_vma=False)
```
